32 devices in a mesh: group: 2 (over x), seq: 16 (over z, y, core).
Axes of the slice: x: 2, y: 2, z: 4, core: 2. Of those that a mesh axis runs over, the one named last changes fastest.
Arguments:
- tokens: bfloat16 [16384, 2048], P(('group', 'seq')), parts along dimension 0, may hold values from -6 to 6
- w_qkv: bfloat16 [2048, 3072], P('seq'), may hold values from -0.125 to 0.125
- w_out: bfloat16 [1024, 2048], P('seq'), may hold values from -0.1875 to 0.1875
- level_weight: float32 [14, 4, 16384], P(None, None, ('group', 'seq')), parts along dimension 2, may hold values from 0.1 to 1
Outputs:
- mixed: bfloat16 [16384, 2048], P(('group', 'seq')), parts along dimension 0
The draws below stay inside these ranges and needn't reach their ends.
There are 2 independent parts, one for each index of `group`. The reference program is written for one: setup_inputs(seed, part) draws one part's arguments, and reference() takes and returns one part's arrays. A program takes and returns all parts, laid end to end along the dimension named above; an argument that names none is the same for every part. Nothing has to cross between parts.
All inputs are finite; a program needn't handle non-finite values.
Results may differ from the reference program's by a relative error of at most 0.0085.
Values may be sent and summed in bfloat16 or wider, within the bound.
A program may use at most 128 MiB of HBM per device.

```python
import math
import jax
import jax.numpy as jnp
from jax import lax

D = 2048
HEADS = 4
HEAD = 256
SPAN = 256
TOKENS = 8192
NCHUNK = 32
CBITS = 8
NBITS = 5
LEVELS = 14


def level_of(stream_key, shape, split, smallest, top_value):
    factor_of, own = 1.0, jax.random.fold_in(stream_key, 6)
    for axis_at, parts in split:
        draws = jnp.exp(jax.random.uniform(jax.random.fold_in(own, axis_at), (parts,), jnp.float32, smallest / len(split), top_value / len(split)))
        factor_of = factor_of * jnp.repeat(draws, shape[axis_at] // parts).reshape([-1 if axis == axis_at else 1 for axis in range(len(shape))])
    return factor_of


def bell_draw(stream_key, shape, width, limit, split=(), held_as=jnp.bfloat16):
    factor_of = level_of(stream_key, shape, split, -0.22, 0.18) if split else 1.0
    entries = jax.random.normal(stream_key, shape, jnp.float32) * width * factor_of
    return jnp.minimum(jnp.maximum(entries, -limit), limit).astype(held_as)


def setup_inputs(seed: int = 0, part: int = 0) -> dict:
    seeds = jax.random.split(jax.random.key(seed), 5)
    own_keys = jax.random.split(jax.random.fold_in(seeds[4], part), 5)
    return {
        "tokens": bell_draw(own_keys[0], (TOKENS, D), 1.0, 6.0, ((0, 16),)),
        "w_qkv": bell_draw(seeds[1], (D, 3 * HEADS * HEAD), D ** -0.5, 0.125, ((0, 16),)),
        "w_out": bell_draw(seeds[2], (HEADS * HEAD, D), (HEADS * HEAD) ** -0.5, 0.1875, ((0, 16),)),
        "level_weight": jnp.clip(jnp.exp(math.log(1.0) - 2.3025851 * jax.random.uniform(own_keys[3], (LEVELS, HEADS, TOKENS), jnp.float32) ** level_of(own_keys[3], (LEVELS, HEADS, TOKENS), ((2, 16),), -0.2, 0.2)), 0.1, 1.0),
    }


def bit_length_of(values):
    result = jnp.zeros(values.shape, jnp.int32)
    for bit_pos in range(24):
        result = result + (values >= 1 << bit_pos).astype(jnp.int32)
    return result

def intra_table(span, cbits, head):
    position = jnp.arange(span, dtype=jnp.int32)
    pair_level = bit_length_of(position[:, None] ^ position[None, :])
    causal = position[:, None] >= position[None, :]
    levels_all = jnp.arange(cbits + 1, dtype=jnp.int32)
    gains = jnp.asarray([1.0 / math.sqrt(head * max(1, 2 ** (level_no - 1))) for level_no in range(cbits + 1)], jnp.float32)
    onehot = ((pair_level[None] == levels_all[:, None, None]) & causal[None]).astype(jnp.float32)
    return onehot * gains[:, None, None]

def reference(tokens, w_qkv, w_out, level_weight):
    highest = lax.Precision.HIGHEST
    head_cols = HEADS * HEAD
    qkv = jnp.dot(tokens, w_qkv, preferred_element_type=jnp.float32).astype(jnp.bfloat16)
    queries = qkv[:, :head_cols].reshape(NCHUNK, SPAN, HEADS, HEAD).astype(jnp.float32)
    key_rows = qkv[:, head_cols:2 * head_cols].reshape(NCHUNK, SPAN, HEADS, HEAD).astype(jnp.float32)
    value_rows = qkv[:, 2 * head_cols:].reshape(NCHUNK, SPAN, HEADS, HEAD).astype(jnp.float32)
    weights = level_weight.reshape(LEVELS, HEADS, NCHUNK, SPAN)
    table = intra_table(SPAN, CBITS, HEAD)
    mixing = jnp.einsum('lij,lhci->chij', table, weights[:CBITS + 1], precision=highest)
    scores = jnp.einsum('cihe,cjhe->chij', queries, key_rows, precision=highest)
    probs = (scores * mixing).astype(jnp.bfloat16)
    probs = lax.optimization_barrier(probs).astype(jnp.float32)
    intra = jnp.einsum('chij,cjhe->cihe', probs, value_rows, precision=highest)
    states = jnp.einsum('cjhe,cjhf->chef', key_rows, value_rows, precision=highest)
    inter = jnp.zeros((NCHUNK, SPAN, HEADS, HEAD), jnp.float32)
    for level_no in range(1, NBITS + 1):
        half_size = 2 ** (level_no - 1)
        blocks = NCHUNK // (2 * half_size)
        left = states.reshape(blocks, 2, half_size, HEADS, HEAD, HEAD)[:, 0].sum(axis=1)
        right_q = queries.reshape(blocks, 2, half_size, SPAN, HEADS, HEAD)[:, 1]
        read = jnp.einsum('bmihe,bhef->bmihf', right_q, left, precision=highest)
        scale = weights[CBITS + level_no].reshape(HEADS, blocks, 2, half_size, SPAN)[:, :, 1]
        scale = jnp.transpose(scale, (1, 2, 3, 0)) * (1.0 / math.sqrt(SPAN * half_size * HEAD))
        shaped = inter.reshape(blocks, 2, half_size, SPAN, HEADS, HEAD)
        inter = shaped.at[:, 1].add(read * scale[..., None]).reshape(NCHUNK, SPAN, HEADS, HEAD)
    attended = (intra + inter).reshape(TOKENS, head_cols).astype(jnp.bfloat16)
    return jnp.dot(attended, w_out, preferred_element_type=jnp.float32).astype(jnp.bfloat16)
```

```python
import functools
import math

import jax
import jax.numpy as jnp
from jax import lax
from jax.experimental import pallas as pl
from jax.experimental.pallas import tpu as pltpu
from jax.sharding import PartitionSpec as P

HEADS = 4
HEAD = 256
SPAN = 256
CBITS = 8
MESH = pl.DeviceIdType.MESH


class Place:
    def __init__(self, groups, seqs):
        self.seqs = seqs
        self.chips = seqs // 2
        self.has_x = groups % 2 == 0
        self.g = lax.axis_index("group")
        self.me = lax.axis_index("seq")
        self.core = lax.rem(self.me, 2)
        self.chip = self.me // 2
        odd = lax.rem(self.chip, 2)
        half = self.chip // 2
        self.pos = half + odd * (self.chips - 1 - 2 * half)
        self.par = lax.rem(self.g, 2)
        self.mate = (self.g, self.me + 1 - 2 * self.core)
        self.cross = (self.g + 1 - 2 * self.par, self.me)

    def chip_at(self, offset):
        pos = lax.rem(self.pos + offset + self.chips, self.chips)
        late = pos // (self.chips // 2)
        return 2 * pos + late * (2 * (self.chips - 1) + 1 - 4 * pos)

    def ring(self, offset):
        return (self.g, self.chip_at(offset) * 2 + self.core)

    def greet(self, others):
        barrier = pltpu.get_barrier_semaphore()
        for other in others:
            pl.semaphore_signal(barrier, inc=1, device_id=other, device_id_type=MESH)
        pl.semaphore_wait(barrier, len(others))

    def neighbours(self):
        found = [self.ring(1), self.ring(-1), self.mate]
        return found + [self.cross] if self.has_x else found


def relay_columns(columns, has_x, share):
    return (columns // share) // 128 * 128 if has_x else 0


class Gather:
    def __init__(self, place, buf, send_sem, recv_sem, share):
        self.at = place
        self.buf = buf
        self.send_sem, self.recv_sem = send_sem, recv_sem
        _, self.rows, self.columns = buf.shape
        self.sub = 2 if self.rows % 32 == 0 else 1
        self.part = self.rows // self.sub
        self.rel = relay_columns(self.columns, place.has_x, share)
        self.slots, self.sent = {}, []
        keep = self.columns - self.rel
        self.ring_cols = (place.par * self.rel, keep) if self.rel else (0, keep)
        self.give_cols = (place.par * keep, self.rel)
        self.take_cols = ((1 - place.par) * keep, self.rel)
        self.last = place.chips // 2

    def view(self, index, h, cols):
        start, width = cols
        if not isinstance(start, int):
            start = pl.multiple_of(start, 128)
        return self.buf.at[index, pl.ds(h * self.part, self.part), pl.ds(start, width)]

    def copy(self, key, index, h, cols, device):
        slot = self.slots.setdefault(key, len(self.slots))
        ref = self.view(index, h, cols)
        return pltpu.make_async_remote_copy(
            src_ref=ref,
            dst_ref=ref,
            send_sem=self.send_sem.at[slot],
            recv_sem=self.recv_sem.at[slot],
            device_id=device,
            device_id_type=MESH,
        )

    def send(self, *args):
        one = self.copy(*args)
        one.start()
        self.sent.append(one)

    def mine(self, offset):
        return self.at.chip_at(offset) * 2 + self.at.core

    def theirs(self, offset):
        return self.at.chip_at(offset) * 2 + 1 - self.at.core

    def pieces(self, step):
        every = [(h, d) for h in range(self.sub) for d in (1, -1)]
        if step < self.last:
            return every
        return [(0, 1), (1, -1)] if self.sub == 2 else [(0, 1)]

    def begin(self):
        for h, d in self.pieces(1):
            self.send(("ring", 1, h, d), self.at.me, h, self.ring_cols, self.at.ring(d))
        for h in range(self.sub):
            self.send(("own", h), self.at.me, h, (0, self.columns), self.at.mate)

    def own(self):
        for h in range(self.sub):
            self.copy(("own", h), self.theirs(0), h, (0, self.columns), self.at.mate).wait_recv()

    def arrive(self, step):
        for h, d in self.pieces(step):
            index = self.mine(-d * step)
            self.copy(("ring", step, h, d), index, h, self.ring_cols, self.at.ring(-d)).wait_recv()
            if step < self.last and (h, d) in self.pieces(step + 1):
                self.send(("ring", step + 1, h, d), index, h, self.ring_cols, self.at.ring(d))
            if step < self.last and self.rel:
                self.send(("cross", step, h, d), index, h, self.give_cols, self.at.cross)
            self.send(("mate", step, h, d), index, h, self.ring_cols, self.at.mate)

    def complete(self, step):
        if self.rel:
            for h, d in self.pieces(step):
                index = self.mine(-d * step)
                if step < self.last:
                    self.copy(("cross", step, h, d), index, h, self.take_cols, self.at.cross).wait_recv()
                    if step + 1 == self.last and (h, d) in self.pieces(step + 1):
                        self.send(("end", h, d), index, h, self.take_cols, self.at.ring(d))
                else:
                    self.copy(("end", h, d), index, h, self.take_cols, self.at.ring(-d)).wait_recv()
                self.send(("pass", step, h, d), index, h, self.take_cols, self.at.mate)
        for h, d in self.pieces(step):
            index = self.theirs(-d * step)
            self.copy(("mate", step, h, d), index, h, self.ring_cols, self.at.mate).wait_recv()
            if self.rel:
                self.copy(("pass", step, h, d), index, h, self.take_cols, self.at.mate).wait_recv()
        return (step, -step) if step < self.last else (step,)

    def run(self, use):
        self.own()
        use(self.at.chip_at(0))
        for step in range(1, self.last):
            self.arrive(step)
            if step > 1:
                for offset in self.complete(step - 1):
                    use(self.at.chip_at(offset))
        for offset in self.complete(self.last - 1):
            use(self.at.chip_at(offset))
        self.arrive(self.last)
        for offset in self.complete(self.last):
            use(self.at.chip_at(offset))

    def drain(self):
        for one in self.sent:
            one.wait_send()


def slots_needed(seqs):
    return 16 * seqs


def project_kernel(groups, seqs, share, tokens_ref, w_ref, out_ref, buf, total, load_sem, send_sem, recv_sem):
    place = Place(groups, seqs)
    load = pltpu.make_async_copy(w_ref, buf.at[place.me], load_sem)
    load.start()
    place.greet(place.neighbours())
    load.wait()
    gather = Gather(place, buf, send_sem, recv_sem, share)
    gather.begin()
    rows, columns = w_ref.shape
    tile = 512
    aligned = (2 * rows) % 128 == 0
    started = []

    def use(chip):
        if not aligned:
            return
        first = not started
        started.append(1)
        x = tokens_ref[:, pl.ds(pl.multiple_of(chip * (2 * rows), 128), 2 * rows)]

        @pl.loop(0, columns // tile)
        def _(t):
            cols = pl.ds(pl.multiple_of(t * tile, tile), tile)
            w = buf[pl.ds(chip * 2, 2), :, cols].reshape(2 * rows, tile)
            y = jnp.dot(x, w, preferred_element_type=jnp.float32)
            if first:
                total[:, cols] = y
            elif len(started) == place.chips:
                out_ref[:, cols] = (total[:, cols] + y).astype(out_ref.dtype)
            else:
                total[:, cols] += y

    gather.run(use)
    if not aligned:

        @pl.loop(0, columns // tile)
        def _(t):
            cols = pl.ds(pl.multiple_of(t * tile, tile), tile)
            w = buf[:, :, cols].reshape(seqs * rows, tile)
            y = jnp.dot(tokens_ref[...], w, preferred_element_type=jnp.float32)
            out_ref[:, cols] = y.astype(out_ref.dtype)

    gather.drain()


def project(tokens, w, groups, seqs):
    rows, columns = w.shape
    count = tokens.shape[0]
    return pl.pallas_call(
        functools.partial(project_kernel, groups, seqs, 3),
        out_shape=jax.ShapeDtypeStruct((count, columns), jnp.bfloat16),
        in_specs=[
            pl.BlockSpec(memory_space=pltpu.VMEM),
            pl.BlockSpec(memory_space=pl.ANY),
        ],
        out_specs=pl.BlockSpec(memory_space=pltpu.VMEM),
        scratch_shapes=[
            pltpu.VMEM((seqs, rows, columns), jnp.bfloat16),
            pltpu.VMEM((count, columns), jnp.float32),
            pltpu.SemaphoreType.DMA,
            pltpu.SemaphoreType.DMA((slots_needed(seqs),)),
            pltpu.SemaphoreType.DMA((slots_needed(seqs),)),
        ],
        compiler_params=pltpu.CompilerParams(
            collective_id=0, has_side_effects=True, vmem_limit_bytes=60 * 1024 * 1024
        ),
    )(tokens, w)


def partner_2(value, axis, bit):
    mask = 2**bit
    pairs = [(source, source ^ mask) for source in range(lax.axis_size(axis))]
    return lax.ppermute(value, axis, pairs)


def bit_length_of(values):
    result = jnp.zeros(values.shape, jnp.int32)
    for bit_pos in range(24):
        result = result + (values >= 1 << bit_pos).astype(jnp.int32)
    return result


def intra_table(span, cbits, head):
    position = jnp.arange(span, dtype=jnp.int32)
    pair_level = bit_length_of(position[:, None] ^ position[None, :])
    causal = position[:, None] >= position[None, :]
    levels_all = jnp.arange(cbits + 1, dtype=jnp.int32)
    gains = jnp.asarray(
        [1.0 / math.sqrt(head * max(1, 2 ** (level_no - 1))) for level_no in range(cbits + 1)],
        jnp.float32,
    )
    onehot = ((pair_level[None] == levels_all[:, None, None]) & causal[None]).astype(jnp.float32)
    return onehot * gains[:, None, None]


def split_read(form, query_half, state):
    return jnp.einsum(form, query_half, state.astype(jnp.bfloat16), preferred_element_type=jnp.float32)


def on_device(tokens, w_qkv, w_out, level_weight):
    highest = lax.Precision.HIGHEST
    head_cols = HEADS * HEAD
    tok_rows = tokens.shape[0]
    count = tok_rows // SPAN
    qkv = project(tokens, w_qkv, lax.axis_size("group"), lax.axis_size("seq"))
    queries = qkv[:, :head_cols].reshape(count, SPAN, HEADS, HEAD)
    key_rows = qkv[:, head_cols : 2 * head_cols].reshape(count, SPAN, HEADS, HEAD)
    value_rows = qkv[:, 2 * head_cols :].reshape(count, SPAN, HEADS, HEAD)
    weights = level_weight.reshape(level_weight.shape[0], HEADS, count, SPAN)
    table = intra_table(SPAN, CBITS, HEAD)
    mixing = jnp.einsum("lij,lhci->chij", table, weights[: CBITS + 1], precision=highest)
    scores = jnp.einsum("cihe,cjhe->chij", queries, key_rows, preferred_element_type=jnp.float32)
    probs = (scores * mixing).astype(jnp.bfloat16)
    intra = jnp.einsum("chij,cjhe->cihe", probs, value_rows, preferred_element_type=jnp.float32)
    states = jnp.einsum("cjhe,cjhf->chef", key_rows, value_rows, preferred_element_type=jnp.float32)
    inter = jnp.zeros((count, SPAN, HEADS, HEAD), jnp.float32)
    local_bits = count.bit_length() - 1
    level_no = 1
    half_size = 2 ** (level_no - 1)
    blocks = count // (2 * half_size)
    left = states.reshape(blocks, 2, half_size, HEADS, HEAD, HEAD)[:, 0].sum(axis=1)
    right_q = queries.reshape(blocks, 2, half_size, SPAN, HEADS, HEAD)[:, 1]
    read = split_read("bmihe,bhef->bmihf", right_q, left)
    scale = weights[CBITS + level_no].reshape(HEADS, blocks, 2, half_size, SPAN)[:, :, 1]
    scale = jnp.transpose(scale, (1, 2, 3, 0)) * (1.0 / math.sqrt(SPAN * half_size * HEAD))
    shaped = inter.reshape(blocks, 2, half_size, SPAN, HEADS, HEAD)
    inter = shaped.at[:, 1].add(read * scale[..., None]).reshape(count, SPAN, HEADS, HEAD)
    block_total = states.sum(axis=0)
    seq_bits = lax.axis_size("seq").bit_length() - 1
    device = lax.axis_index("seq")
    for bit_pos in range(seq_bits):
        upper = (device >> bit_pos & 1).astype(jnp.float32)
        partner = partner_2(block_total.astype(jnp.bfloat16), "seq", bit_pos)
        level_no = local_bits + bit_pos + 1
        gain = 1.0 / math.sqrt(SPAN * 2 ** (level_no - 1) * HEAD)
        level_scale = jnp.transpose(weights[CBITS + level_no], (1, 2, 0)) * (upper * gain)
        single = split_read("cihe,hef->cihf", queries, partner)
        inter = inter + single * level_scale[..., None]
        if bit_pos + 1 < seq_bits:
            block_total = block_total + partner
    attended = (intra + inter).reshape(tok_rows, head_cols).astype(jnp.bfloat16)
    columns = attended
    mixed = jnp.dot(
        columns,
        lax.all_gather(w_out, "seq", axis=0, tiled=True),
        preferred_element_type=jnp.float32,
    )
    return mixed.astype(jnp.bfloat16)


def solution(mesh):
    return jax.shard_map(
        on_device,
        mesh=mesh,
        in_specs=(
            P(("group", "seq"), None),
            P("seq", None),
            P("seq", None),
            P(None, None, ("group", "seq")),
        ),
        out_specs=P(("group", "seq"), None),
        check_vma=False,
    )
```

```python
import functools
import math

import jax
import jax.numpy as jnp
from jax import lax
from jax.experimental import pallas as pl
from jax.experimental.pallas import tpu as pltpu
from jax.sharding import PartitionSpec as P

HEADS = 4
HEAD = 256
SPAN = 256
CBITS = 8
MESH = pl.DeviceIdType.MESH


class Place:
    def __init__(self, groups, seqs):
        self.seqs = seqs
        self.chips = seqs // 2
        self.has_x = groups % 2 == 0
        self.g = lax.axis_index("group")
        self.me = lax.axis_index("seq")
        self.core = lax.rem(self.me, 2)
        self.chip = self.me // 2
        odd = lax.rem(self.chip, 2)
        half = self.chip // 2
        self.pos = half + odd * (self.chips - 1 - 2 * half)
        self.par = lax.rem(self.g, 2)
        self.mate = (self.g, self.me + 1 - 2 * self.core)
        self.cross = (self.g + 1 - 2 * self.par, self.me)

    def chip_at(self, offset):
        pos = lax.rem(self.pos + offset + self.chips, self.chips)
        late = pos // (self.chips // 2)
        return 2 * pos + late * (2 * (self.chips - 1) + 1 - 4 * pos)

    def ring(self, offset):
        return (self.g, self.chip_at(offset) * 2 + self.core)

    def flip(self, bit):
        return (self.g, self.me + (1 - 2 * self.digit(bit)) * 2**bit)

    def digit(self, bit):
        return lax.rem(self.me // 2**bit, 2)

    def greet(self, others):
        barrier = pltpu.get_barrier_semaphore()
        for other in others:
            pl.semaphore_signal(barrier, inc=1, device_id=other, device_id_type=MESH)
        pl.semaphore_wait(barrier, len(others))

    def neighbours(self):
        found = [self.ring(1), self.ring(-1), self.mate]
        return found + [self.cross] if self.has_x else found


def relay_columns(columns, has_x, share):
    return (columns // share) // 128 * 128 if has_x else 0


class Gather:
    def __init__(self, place, buf, send_sem, recv_sem, share):
        self.at = place
        self.buf = buf
        self.send_sem, self.recv_sem = send_sem, recv_sem
        _, self.rows, self.columns = buf.shape
        self.sub = 2 if self.rows % 32 == 0 else 1
        self.part = self.rows // self.sub
        self.rel = relay_columns(self.columns, place.has_x, share)
        self.slots, self.sent = {}, []
        keep = self.columns - self.rel
        self.ring_cols = (place.par * self.rel, keep) if self.rel else (0, keep)
        self.give_cols = (place.par * keep, self.rel)
        self.take_cols = ((1 - place.par) * keep, self.rel)
        self.last = place.chips // 2

    def view(self, index, h, cols):
        start, width = cols
        if not isinstance(start, int):
            start = pl.multiple_of(start, 128)
        return self.buf.at[index, pl.ds(h * self.part, self.part), pl.ds(start, width)]

    def copy(self, key, index, h, cols, device):
        slot = self.slots.setdefault(key, len(self.slots))
        ref = self.view(index, h, cols)
        return pltpu.make_async_remote_copy(
            src_ref=ref,
            dst_ref=ref,
            send_sem=self.send_sem.at[slot],
            recv_sem=self.recv_sem.at[slot],
            device_id=device,
            device_id_type=MESH,
        )

    def send(self, *args):
        one = self.copy(*args)
        one.start()
        self.sent.append(one)

    def mine(self, offset):
        return self.at.chip_at(offset) * 2 + self.at.core

    def theirs(self, offset):
        return self.at.chip_at(offset) * 2 + 1 - self.at.core

    def pieces(self, step):
        every = [(h, d) for h in range(self.sub) for d in (1, -1)]
        if step < self.last:
            return every
        return [(0, 1), (1, -1)] if self.sub == 2 else [(0, 1)]

    def begin(self):
        for h, d in self.pieces(1):
            self.send(("ring", 1, h, d), self.at.me, h, self.ring_cols, self.at.ring(d))
        for h in range(self.sub):
            self.send(("own", h), self.at.me, h, (0, self.columns), self.at.mate)

    def own(self):
        for h in range(self.sub):
            self.copy(("own", h), self.theirs(0), h, (0, self.columns), self.at.mate).wait_recv()

    def arrive(self, step):
        for h, d in self.pieces(step):
            index = self.mine(-d * step)
            self.copy(("ring", step, h, d), index, h, self.ring_cols, self.at.ring(-d)).wait_recv()
            if step < self.last and (h, d) in self.pieces(step + 1):
                self.send(("ring", step + 1, h, d), index, h, self.ring_cols, self.at.ring(d))
            if step < self.last and self.rel:
                self.send(("cross", step, h, d), index, h, self.give_cols, self.at.cross)
            self.send(("mate", step, h, d), index, h, self.ring_cols, self.at.mate)

    def complete(self, step):
        if self.rel:
            for h, d in self.pieces(step):
                index = self.mine(-d * step)
                if step < self.last:
                    self.copy(("cross", step, h, d), index, h, self.take_cols, self.at.cross).wait_recv()
                    if step + 1 == self.last and (h, d) in self.pieces(step + 1):
                        self.send(("end", h, d), index, h, self.take_cols, self.at.ring(d))
                else:
                    self.copy(("end", h, d), index, h, self.take_cols, self.at.ring(-d)).wait_recv()
                self.send(("pass", step, h, d), index, h, self.take_cols, self.at.mate)
        for h, d in self.pieces(step):
            index = self.theirs(-d * step)
            self.copy(("mate", step, h, d), index, h, self.ring_cols, self.at.mate).wait_recv()
            if self.rel:
                self.copy(("pass", step, h, d), index, h, self.take_cols, self.at.mate).wait_recv()
        return (step, -step) if step < self.last else (step,)

    def run(self, use, before_end):
        self.own()
        use(self.at.chip_at(0))
        for step in range(1, self.last):
            self.arrive(step)
            if step > 1:
                for offset in self.complete(step - 1):
                    use(self.at.chip_at(offset))
        for offset in self.complete(self.last - 1):
            use(self.at.chip_at(offset))
        self.arrive(self.last)
        before_end()
        for offset in self.complete(self.last):
            use(self.at.chip_at(offset))

    def drain(self):
        for one in self.sent:
            one.wait_send()


def slots_needed(seqs):
    return 4 * seqs + 8


class Exchange:
    def __init__(self, place, left, send_sem, recv_sem):
        self.at, self.left = place, left
        self.send_sem, self.recv_sem = send_sem, recv_sem
        self.slots, self.sent = {}, []
        self.c, self.y = place.core, place.digit(1)
        self.head = 2 * self.c + self.y
        self.other = 2 * self.c + 1 - self.y
        self.mate_head = 2 * (1 - self.c) + self.y
        self.mate_other = 2 * (1 - self.c) + 1 - self.y

    def copy(self, key, src, bit, head, device):
        slot = self.slots.setdefault(key, len(self.slots))
        return pltpu.make_async_remote_copy(
            src_ref=src,
            dst_ref=self.left.at[bit, head],
            send_sem=self.send_sem.at[slot],
            recv_sem=self.recv_sem.at[slot],
            device_id=device,
            device_id_type=MESH,
        )

    def send(self, *args):
        one = self.copy(*args)
        one.start()
        self.sent.append(one)

    def forward(self, key, bit, head, device):
        self.send(key, self.left.at[bit, head], bit, head, device)

    def wait(self, key, bit, head, device):
        self.copy(key, self.left.at[bit, head], bit, head, device).wait_recv()

    def spread(self, bit):
        self.forward(("quad", bit), bit, self.head, self.at.flip(1))
        self.forward(("near", bit), bit, self.head, self.at.mate)

    def collect(self, bit):
        if bit > 1:
            self.wait(("quad", bit), bit, self.other, self.at.flip(1))
        else:
            self.wait(("across", 1), bit, self.other, self.at.flip(1))
        self.forward(("far", bit), bit, self.other, self.at.mate)
        self.wait(("near", bit), bit, self.mate_head, self.at.mate)
        self.wait(("far", bit), bit, self.mate_other, self.at.mate)

    def drain(self):
        for one in self.sent:
            one.wait_send()


def product(a, b, dims):
    return lax.dot_general(a, b, (dims, ((), ())), preferred_element_type=jnp.float32)


def head_cols(h):
    return pl.ds(h * HEAD, HEAD)


def layer_kernel(
    groups, seqs, tokens_ref, w_ref, wo_ref, weight_ref, out_ref,
    buf, total, qkv, wo_buf, mix, acc, attended, local_sum, first_sum, give, pair, pair_give, run_give, left,
    load_sem, send_sem, recv_sem, wo_send, wo_recv, ex_send, ex_recv,
):
    place = Place(groups, seqs)
    load = pltpu.make_async_copy(w_ref, buf.at[place.me], load_sem.at[0])
    load.start()
    load_o = pltpu.make_async_copy(wo_ref, wo_buf.at[place.me], load_sem.at[1])
    load_o.start()
    seq_bits = seqs.bit_length() - 1
    place.greet(place.neighbours() + [place.flip(b) for b in range(1, seq_bits)])
    load.wait()
    gather = Gather(place, buf, send_sem, recv_sem, 3)
    gather.begin()
    load_o.wait()
    gather_o = Gather(place, wo_buf, wo_send, wo_recv, 3)

    count = tokens_ref.shape[0] // SPAN
    wide = HEADS * HEAD

    @pl.loop(0, count)
    def _(c):
        rows = pl.ds(pl.multiple_of(c * SPAN, SPAN), SPAN)
        i = lax.broadcasted_iota(jnp.int32, (SPAN, SPAN), 0)
        j = lax.broadcasted_iota(jnp.int32, (SPAN, SPAN), 1)
        apart = i ^ j
        for h in range(HEADS):
            value = jnp.zeros((SPAN, SPAN), jnp.float32)
            for level in range(CBITS + 1):
                gain = 1.0 / math.sqrt(HEAD * max(1, 2 ** (level - 1)))
                column = weight_ref[rows, level * HEADS + h : level * HEADS + h + 1] * gain
                column = jnp.broadcast_to(column, (SPAN, SPAN))
                value = column if level == 0 else jnp.where(apart >= 2 ** (level - 1), column, value)
            mix[c, h] = jnp.where(i >= j, value, 0.0)

    rows_w, columns = w_ref.shape
    tile = 512
    aligned = (2 * rows_w) % 128 == 0
    started = []

    def use(chip):
        if not aligned:
            return
        started.append(1)
        step = len(started)
        x = tokens_ref[:, pl.ds(pl.multiple_of(chip * (2 * rows_w), 128), 2 * rows_w)]

        @pl.loop(0, columns // tile)
        def _(t):
            cols = pl.ds(pl.multiple_of(t * tile, tile), tile)
            w = buf[pl.ds(chip * 2, 2), :, cols].reshape(2 * rows_w, tile)
            y = jnp.dot(x, w, preferred_element_type=jnp.float32)
            if step == 1:
                total[:, cols] = y
            elif step == place.chips:
                qkv[:, cols] = (total[:, cols] + y).astype(qkv.dtype)
            else:
                total[:, cols] += y

    gather.run(use, gather_o.begin)
    if not aligned:

        @pl.loop(0, columns // tile)
        def _(t):
            cols = pl.ds(pl.multiple_of(t * tile, tile), tile)
            w = buf[:, :, cols].reshape(seqs * rows_w, tile)
            y = jnp.dot(tokens_ref[...], w, preferred_element_type=jnp.float32)
            qkv[:, cols] = y.astype(qkv.dtype)

    for h in range(HEADS):
        for c in range(count):
            k = qkv[pl.ds(c * SPAN, SPAN), head_cols(HEADS + h)]
            v = qkv[pl.ds(c * SPAN, SPAN), head_cols(2 * HEADS + h)]
            state = product(k, v, ((0,), (0,)))
            if c == 0:
                local_sum[h] = state
                first_sum[h] = state.astype(jnp.bfloat16)
            else:
                local_sum[h] += state
        give[h] = local_sum[h].astype(jnp.bfloat16)
    exchange = Exchange(place, left, ex_send, ex_recv)
    for h in range(HEADS):
        exchange.send(("core", h), give.at[h], 0, h, place.mate)

    def attend(c):
        rows = pl.ds(c * SPAN, SPAN)
        for h in range(HEADS):
            q = qkv[rows, head_cols(h)]
            k = qkv[rows, head_cols(HEADS + h)]
            v = qkv[rows, head_cols(2 * HEADS + h)]
            scores = product(q, k, ((1,), (1,)))
            probs = (scores * mix[c, h]).astype(jnp.bfloat16)
            acc[rows, head_cols(h)] = product(probs, v, ((1,), (0,)))

    def gain_of(level):
        return 1.0 / math.sqrt(SPAN * 2 ** (level - 1) * HEAD)

    def weight_of(rows, level, h):
        at = (CBITS + level) * HEADS + h
        return weight_ref[rows, at : at + 1]

    def read(bit):
        level = local_bits + bit + 1
        scale = place.digit(bit).astype(jnp.float32) * gain_of(level)
        every = pl.ds(0, count * SPAN)
        for h in range(HEADS):
            got = product(qkv[:, head_cols(h)], left[bit, h], ((1,), (0,)))
            acc[:, head_cols(h)] += got * (weight_of(every, level, h) * scale)

    local_bits = count.bit_length() - 1
    attend(0)
    gather_o.own()
    gather_o.arrive(1)
    for h in range(HEADS):
        exchange.wait(("core", h), 0, h, place.mate)
    for n in range(2):
        h = 2 * place.core + n
        pair[n] = local_sum[h] + left[0, h].astype(jnp.float32)
        pair_give[n] = pair[n].astype(jnp.bfloat16)
    y = place.digit(1)
    for n, which in enumerate((1 - y, y)):
        exchange.send(("across", n), pair_give.at[which], 1, 2 * place.core + which, place.flip(1))
    for c in range(1, count):
        attend(c)
    for c in range(1, count):
        rows = pl.ds(c * SPAN, SPAN)
        for h in range(HEADS):
            got = product(qkv[rows, head_cols(h)], first_sum[h], ((1,), (0,)))
            acc[rows, head_cols(h)] += got * (weight_of(rows, 1, h) * gain_of(1))
    steps = iter(range(2, gather_o.last + 1))
    done_o = [1]

    def advance():
        step = next(steps, None)
        if step is not None:
            if step == gather_o.last:
                gather_o.complete(step - 1)
                gather_o.arrive(step)
            else:
                gather_o.arrive(step)
                gather_o.complete(step - 1)
            done_o.append(step)

    exchange.wait(("across", 0), 1, exchange.head, place.flip(1))
    running = pair[y] + left[1, exchange.head].astype(jnp.float32)
    exchange.forward(("near", 1), 1, exchange.head, place.mate)
    for bit in range(2, seq_bits):
        run_give[bit] = running.astype(jnp.bfloat16)
        exchange.send(("hop", bit), run_give.at[bit], bit, exchange.head, place.flip(bit))
        exchange.collect(bit - 1)
        advance()
        read(bit - 2)
        exchange.wait(("hop", bit), bit, exchange.head, place.flip(bit))
        exchange.spread(bit)
        if bit + 1 < seq_bits:
            running = running + left[bit, exchange.head].astype(jnp.float32)
    read(seq_bits - 2)
    while done_o[-1] < gather_o.last:
        advance()
    exchange.collect(seq_bits - 1)
    gather_o.complete(gather_o.last)
    read(seq_bits - 1)

    attended[...] = acc[...].astype(jnp.bfloat16)

    @pl.loop(0, wo_ref.shape[1] // tile)
    def _(t):
        cols = pl.ds(pl.multiple_of(t * tile, tile), tile)
        w = wo_buf[:, :, cols].reshape(wide, tile)
        out_ref[:, cols] = jnp.dot(
            attended[...], w, preferred_element_type=jnp.float32
        ).astype(out_ref.dtype)

    gather.drain()
    gather_o.drain()
    exchange.drain()


def on_device(tokens, w_qkv, w_out, level_weight):
    groups, seqs = lax.axis_size("group"), lax.axis_size("seq")
    rows = tokens.shape[0]
    count = rows // SPAN
    seq_bits = seqs.bit_length() - 1
    weights = level_weight.reshape(-1, rows).T
    square = (HEAD, HEAD)
    vmem = pl.BlockSpec(memory_space=pltpu.VMEM)
    hbm = pl.BlockSpec(memory_space=pl.ANY)
    sems = pltpu.SemaphoreType.DMA((slots_needed(seqs),))
    return pl.pallas_call(
        functools.partial(layer_kernel, groups, seqs),
        out_shape=jax.ShapeDtypeStruct((rows, w_out.shape[1]), jnp.bfloat16),
        in_specs=[vmem, hbm, hbm, vmem],
        out_specs=vmem,
        scratch_shapes=[
            pltpu.VMEM((seqs, *w_qkv.shape), jnp.bfloat16),
            pltpu.VMEM((rows, w_qkv.shape[1]), jnp.float32),
            pltpu.VMEM((rows, w_qkv.shape[1]), jnp.bfloat16),
            pltpu.VMEM((seqs, *w_out.shape), jnp.bfloat16),
            pltpu.VMEM((count, HEADS, SPAN, SPAN), jnp.float32),
            pltpu.VMEM((rows, HEADS * HEAD), jnp.float32),
            pltpu.VMEM((rows, HEADS * HEAD), jnp.bfloat16),
            pltpu.VMEM((HEADS, *square), jnp.float32),
            pltpu.VMEM((HEADS, *square), jnp.bfloat16),
            pltpu.VMEM((HEADS, *square), jnp.bfloat16),
            pltpu.VMEM((2, *square), jnp.float32),
            pltpu.VMEM((2, *square), jnp.bfloat16),
            pltpu.VMEM((seq_bits, *square), jnp.bfloat16),
            pltpu.VMEM((seq_bits, HEADS, *square), jnp.bfloat16),
            pltpu.SemaphoreType.DMA((2,)),
            sems, sems, sems, sems,
            pltpu.SemaphoreType.DMA((8 * seq_bits,)),
            pltpu.SemaphoreType.DMA((8 * seq_bits,)),
        ],
        compiler_params=pltpu.CompilerParams(
            collective_id=0, has_side_effects=True, vmem_limit_bytes=63 * 1024 * 1024
        ),
    )(tokens, w_qkv, w_out, weights)


def solution(mesh):
    return jax.shard_map(
        on_device,
        mesh=mesh,
        in_specs=(
            P(("group", "seq"), None),
            P("seq", None),
            P("seq", None),
            P(None, None, ("group", "seq")),
        ),
        out_specs=P(("group", "seq"), None),
        check_vma=False,
    )
```

```python
import functools
import math

import jax
import jax.numpy as jnp
from jax import lax
from jax.experimental import pallas as pl
from jax.experimental.pallas import tpu as pltpu
from jax.sharding import PartitionSpec as P

HEADS = 4
HEAD = 256
SPAN = 256
CBITS = 8
MESH = pl.DeviceIdType.MESH


class Place:
    def __init__(self, groups, seqs):
        self.seqs = seqs
        self.chips = seqs // 2
        self.has_x = groups % 2 == 0
        self.g = lax.axis_index("group")
        self.me = lax.axis_index("seq")
        self.core = lax.rem(self.me, 2)
        self.chip = self.me // 2
        odd = lax.rem(self.chip, 2)
        half = self.chip // 2
        self.pos = half + odd * (self.chips - 1 - 2 * half)
        self.par = lax.rem(self.g, 2)
        self.mate = (self.g, self.me + 1 - 2 * self.core)
        self.cross = (self.g + 1 - 2 * self.par, self.me)

    def chip_at(self, offset):
        pos = lax.rem(self.pos + offset + self.chips, self.chips)
        late = pos // (self.chips // 2)
        return 2 * pos + late * (2 * (self.chips - 1) + 1 - 4 * pos)

    def ring(self, offset):
        return (self.g, self.chip_at(offset) * 2 + self.core)

    def flip(self, bit):
        return (self.g, self.me + (1 - 2 * self.digit(bit)) * 2**bit)

    def digit(self, bit):
        return lax.rem(self.me // 2**bit, 2)

    def greet(self, others):
        barrier = pltpu.get_barrier_semaphore()
        for other in others:
            pl.semaphore_signal(barrier, inc=1, device_id=other, device_id_type=MESH)
        pl.semaphore_wait(barrier, len(others))

    def neighbours(self):
        found = [self.ring(1), self.ring(-1), self.mate]
        return found + [self.cross] if self.has_x else found


def relay_columns(columns, has_x, share):
    return (columns // share) // 128 * 128 if has_x else 0


class Gather:
    def __init__(self, place, buf, send_sem, recv_sem, share):
        self.at = place
        self.buf = buf
        self.send_sem, self.recv_sem = send_sem, recv_sem
        _, self.rows, self.columns = buf.shape
        self.sub = 2 if self.rows % 32 == 0 else 1
        self.part = self.rows // self.sub
        self.rel = relay_columns(self.columns, place.has_x, share)
        self.slots, self.sent = {}, []
        keep = self.columns - self.rel
        self.ring_cols = (place.par * self.rel, keep) if self.rel else (0, keep)
        self.give_cols = (place.par * keep, self.rel)
        self.take_cols = ((1 - place.par) * keep, self.rel)
        self.last = place.chips // 2

    def view(self, index, h, cols):
        start, width = cols
        if not isinstance(start, int):
            start = pl.multiple_of(start, 128)
        return self.buf.at[index, pl.ds(h * self.part, self.part), pl.ds(start, width)]

    def copy(self, key, index, h, cols, device):
        slot = self.slots.setdefault(key, len(self.slots))
        ref = self.view(index, h, cols)
        return pltpu.make_async_remote_copy(
            src_ref=ref,
            dst_ref=ref,
            send_sem=self.send_sem.at[slot],
            recv_sem=self.recv_sem.at[slot],
            device_id=device,
            device_id_type=MESH,
        )

    def send(self, *args):
        one = self.copy(*args)
        one.start()
        self.sent.append(one)

    def mine(self, offset):
        return self.at.chip_at(offset) * 2 + self.at.core

    def theirs(self, offset):
        return self.at.chip_at(offset) * 2 + 1 - self.at.core

    def pieces(self, step):
        every = [(h, d) for h in range(self.sub) for d in (1, -1)]
        if step < self.last:
            return every
        return [(0, 1), (1, -1)] if self.sub == 2 else [(0, 1)]

    def begin(self):
        for h, d in self.pieces(1):
            self.send(("ring", 1, h, d), self.at.me, h, self.ring_cols, self.at.ring(d))
        for h in range(self.sub):
            self.send(("own", h), self.at.me, h, (0, self.columns), self.at.mate)

    def own(self):
        for h in range(self.sub):
            self.copy(("own", h), self.theirs(0), h, (0, self.columns), self.at.mate).wait_recv()

    def arrive(self, step):
        for h, d in self.pieces(step):
            index = self.mine(-d * step)
            self.copy(("ring", step, h, d), index, h, self.ring_cols, self.at.ring(-d)).wait_recv()
            if step < self.last and (h, d) in self.pieces(step + 1):
                self.send(("ring", step + 1, h, d), index, h, self.ring_cols, self.at.ring(d))
            if step < self.last and self.rel:
                self.send(("cross", step, h, d), index, h, self.give_cols, self.at.cross)
            self.send(("mate", step, h, d), index, h, self.ring_cols, self.at.mate)

    def complete(self, step):
        if self.rel:
            for h, d in self.pieces(step):
                index = self.mine(-d * step)
                if step < self.last:
                    self.copy(("cross", step, h, d), index, h, self.take_cols, self.at.cross).wait_recv()
                    if step + 1 == self.last and (h, d) in self.pieces(step + 1):
                        self.send(("end", h, d), index, h, self.take_cols, self.at.ring(d))
                else:
                    self.copy(("end", h, d), index, h, self.take_cols, self.at.ring(-d)).wait_recv()
                self.send(("pass", step, h, d), index, h, self.take_cols, self.at.mate)
        for h, d in self.pieces(step):
            index = self.theirs(-d * step)
            self.copy(("mate", step, h, d), index, h, self.ring_cols, self.at.mate).wait_recv()
            if self.rel:
                self.copy(("pass", step, h, d), index, h, self.take_cols, self.at.mate).wait_recv()
        return (step, -step) if step < self.last else (step,)

    def steps(self, use, before_end):
        self.own()
        use(self.at.chip_at(0))
        for step in range(1, self.last):
            self.arrive(step)
            if step > 1:
                for offset in self.complete(step - 1):
                    use(self.at.chip_at(offset))
            yield
        for offset in self.complete(self.last - 1):
            use(self.at.chip_at(offset))
        self.arrive(self.last)
        before_end()
        yield
        for offset in self.complete(self.last):
            use(self.at.chip_at(offset))

    def drain(self):
        for one in self.sent:
            one.wait_send()


def slots_needed(seqs):
    return 4 * seqs + 8


class Exchange:
    def __init__(self, place, left, send_sem, recv_sem):
        self.at, self.left = place, left
        self.send_sem, self.recv_sem = send_sem, recv_sem
        self.slots, self.sent = {}, []
        self.c, self.y = place.core, place.digit(1)
        self.head = 2 * self.c + self.y
        self.other = 2 * self.c + 1 - self.y
        self.mate_head = 2 * (1 - self.c) + self.y
        self.mate_other = 2 * (1 - self.c) + 1 - self.y

    def copy(self, key, src, bit, head, device):
        slot = self.slots.setdefault(key, len(self.slots))
        return pltpu.make_async_remote_copy(
            src_ref=src,
            dst_ref=self.left.at[bit, head],
            send_sem=self.send_sem.at[slot],
            recv_sem=self.recv_sem.at[slot],
            device_id=device,
            device_id_type=MESH,
        )

    def send(self, *args):
        one = self.copy(*args)
        one.start()
        self.sent.append(one)

    def forward(self, key, bit, head, device):
        self.send(key, self.left.at[bit, head], bit, head, device)

    def wait(self, key, bit, head, device):
        self.copy(key, self.left.at[bit, head], bit, head, device).wait_recv()

    def spread(self, bit):
        self.forward(("quad", bit), bit, self.head, self.at.flip(1))
        self.forward(("near", bit), bit, self.head, self.at.mate)

    def collect(self, bit):
        if bit > 1:
            self.wait(("quad", bit), bit, self.other, self.at.flip(1))
        else:
            self.wait(("across", 1), bit, self.other, self.at.flip(1))
        self.forward(("far", bit), bit, self.other, self.at.mate)
        self.wait(("near", bit), bit, self.mate_head, self.at.mate)
        self.wait(("far", bit), bit, self.mate_other, self.at.mate)

    def drain(self):
        for one in self.sent:
            one.wait_send()


def product(a, b, dims):
    return lax.dot_general(a, b, (dims, ((), ())), preferred_element_type=jnp.float32)


def head_cols(h):
    return pl.ds(h * HEAD, HEAD)


def layer_kernel(
    groups, seqs, tokens_hbm, w_ref, wo_ref, weight_ref, out_ref,
    tokens_ref, kv_buf, q_buf, wo_buf, total, qkv, mix, acc, attended, local_sum, first_sum, give, pair, pair_give,
    run_give, left, load_sem, kv_send, kv_recv, q_send, q_recv, wo_send, wo_recv, ex_send, ex_recv,
):
    place = Place(groups, seqs)
    rows_w, columns = w_ref.shape
    wide = HEADS * HEAD
    here = place.me
    loads = [
        pltpu.make_async_copy(src, dst, load_sem.at[n])
        for n, (src, dst) in enumerate(
            (
                (w_ref.at[:, pl.ds(wide, columns - wide)], kv_buf.at[here]),
                (w_ref.at[:, pl.ds(0, wide)], q_buf.at[here]),
                (wo_ref, wo_buf.at[here]),
                (tokens_hbm, tokens_ref),
            )
        )
    ]
    for one in loads:
        one.start()
    seq_bits = seqs.bit_length() - 1
    place.greet(place.neighbours() + [place.flip(b) for b in range(1, seq_bits)])
    loads[0].wait()
    gather_kv = Gather(place, kv_buf, kv_send, kv_recv, 3)
    gather_kv.begin()
    for one in loads[1:]:
        one.wait()
    gather_q = Gather(place, q_buf, q_send, q_recv, 3)
    gather_o = Gather(place, wo_buf, wo_send, wo_recv, 3)

    count = tokens_ref.shape[0] // SPAN

    @pl.loop(0, count)
    def _(c):
        rows = pl.ds(pl.multiple_of(c * SPAN, SPAN), SPAN)
        i = lax.broadcasted_iota(jnp.int32, (SPAN, SPAN), 0)
        j = lax.broadcasted_iota(jnp.int32, (SPAN, SPAN), 1)
        apart = i ^ j
        for h in range(HEADS):
            value = jnp.zeros((SPAN, SPAN), jnp.float32)
            for level in range(CBITS + 1):
                gain = 1.0 / math.sqrt(HEAD * max(1, 2 ** (level - 1)))
                column = weight_ref[rows, level * HEADS + h : level * HEADS + h + 1] * gain
                column = jnp.broadcast_to(column, (SPAN, SPAN))
                value = column if level == 0 else jnp.where(apart >= 2 ** (level - 1), column, value)
            mix[c, h] = jnp.where(i >= j, value, 0.0)

    tile = 512
    aligned = (2 * rows_w) % 128 == 0

    def user(buf, base):
        started = []

        def use(chip):
            if not aligned:
                return
            started.append(1)
            step = len(started)
            x = tokens_ref[:, pl.ds(pl.multiple_of(chip * (2 * rows_w), 128), 2 * rows_w)]

            @pl.loop(0, buf.shape[2] // tile)
            def _(t):
                cols = pl.ds(pl.multiple_of(t * tile, tile), tile)
                w = buf[pl.ds(chip * 2, 2), :, cols].reshape(2 * rows_w, tile)
                y = jnp.dot(x, w, preferred_element_type=jnp.float32)
                if step == 1:
                    total[:, cols] = y
                elif step == place.chips:
                    qkv[:, pl.ds(pl.multiple_of(base + t * tile, tile), tile)] = (total[:, cols] + y).astype(qkv.dtype)
                else:
                    total[:, cols] += y

        return use

    def at_once(buf, base):
        if aligned:
            return

        @pl.loop(0, buf.shape[2] // tile)
        def _(t):
            cols = pl.ds(pl.multiple_of(t * tile, tile), tile)
            w = buf[:, :, cols].reshape(seqs * rows_w, tile)
            y = jnp.dot(tokens_ref[...], w, preferred_element_type=jnp.float32)
            qkv[:, pl.ds(pl.multiple_of(base + t * tile, tile), tile)] = y.astype(qkv.dtype)

    for _ in gather_kv.steps(user(kv_buf, wide), gather_q.begin):
        pass
    at_once(kv_buf, wide)

    for h in range(HEADS):
        for c in range(count):
            k = qkv[pl.ds(c * SPAN, SPAN), head_cols(HEADS + h)]
            v = qkv[pl.ds(c * SPAN, SPAN), head_cols(2 * HEADS + h)]
            state = product(k, v, ((0,), (0,)))
            if c == 0:
                local_sum[h] = state
                first_sum[h] = state.astype(jnp.bfloat16)
            else:
                local_sum[h] += state
        give[h] = local_sum[h].astype(jnp.bfloat16)
    exchange = Exchange(place, left, ex_send, ex_recv)
    for h in range(HEADS):
        exchange.send(("core", h), give.at[h], 0, h, place.mate)

    def exchange_steps():
        for h in range(HEADS):
            exchange.wait(("core", h), 0, h, place.mate)
        for n in range(2):
            h = 2 * place.core + n
            pair[n] = local_sum[h] + left[0, h].astype(jnp.float32)
            pair_give[n] = pair[n].astype(jnp.bfloat16)
        y = place.digit(1)
        for n, which in enumerate((1 - y, y)):
            exchange.send(("across", n), pair_give.at[which], 1, 2 * place.core + which, place.flip(1))
        yield
        exchange.wait(("across", 0), 1, exchange.head, place.flip(1))
        running = pair[y] + left[1, exchange.head].astype(jnp.float32)
        run_give[2] = running.astype(jnp.bfloat16)
        exchange.send(("hop", 2), run_give.at[2], 2, exchange.head, place.flip(2))
        exchange.forward(("near", 1), 1, exchange.head, place.mate)
        yield
        for bit in range(2, seq_bits):
            exchange.wait(("hop", bit), bit, exchange.head, place.flip(bit))
            if bit + 1 < seq_bits:
                running = running + left[bit, exchange.head].astype(jnp.float32)
                run_give[bit + 1] = running.astype(jnp.bfloat16)
                exchange.send(("hop", bit + 1), run_give.at[bit + 1], bit + 1, exchange.head, place.flip(bit + 1))
            exchange.spread(bit)
            exchange.collect(bit - 1)
            yield
        exchange.collect(seq_bits - 1)

    stages = exchange_steps()
    for _ in gather_q.steps(user(q_buf, 0), gather_o.begin):
        next(stages, None)
    at_once(q_buf, 0)

    local_bits = count.bit_length() - 1

    def gain_of(level):
        return 1.0 / math.sqrt(SPAN * 2 ** (level - 1) * HEAD)

    def weight_of(rows, level, h):
        at = (CBITS + level) * HEADS + h
        return weight_ref[rows, at : at + 1]

    def attend(c):
        rows = pl.ds(c * SPAN, SPAN)
        for h in range(HEADS):
            q = qkv[rows, head_cols(h)]
            k = qkv[rows, head_cols(HEADS + h)]
            v = qkv[rows, head_cols(2 * HEADS + h)]
            scores = product(q, k, ((1,), (1,)))
            probs = (scores * mix[c, h]).astype(jnp.bfloat16)
            got = product(probs, v, ((1,), (0,)))
            if c > 0:
                got += product(q, first_sum[h], ((1,), (0,))) * (weight_of(rows, 1, h) * gain_of(1))
            acc[rows, head_cols(h)] = got

    def read(bit):
        level = local_bits + bit + 1
        scale = place.digit(bit).astype(jnp.float32) * gain_of(level)
        every = pl.ds(0, count * SPAN)
        for h in range(HEADS):
            got = product(qkv[:, head_cols(h)], left[bit, h], ((1,), (0,)))
            acc[:, head_cols(h)] += got * (weight_of(every, level, h) * scale)

    work = [functools.partial(attend, c) for c in range(count)]
    for _ in gather_o.steps(lambda chip: None, lambda: None):
        if work:
            work.pop(0)()
        next(stages, None)
    for one in work:
        one()
    for _ in stages:
        pass
    for bit in range(seq_bits):
        read(bit)

    attended[...] = acc[...].astype(jnp.bfloat16)

    @pl.loop(0, wo_ref.shape[1] // tile)
    def _(t):
        cols = pl.ds(pl.multiple_of(t * tile, tile), tile)
        w = wo_buf[:, :, cols].reshape(wide, tile)
        out_ref[:, cols] = jnp.dot(
            attended[...], w, preferred_element_type=jnp.float32
        ).astype(out_ref.dtype)

    for one in (gather_kv, gather_q, gather_o, exchange):
        one.drain()


def on_device(tokens, w_qkv, w_out, level_weight):
    groups, seqs = lax.axis_size("group"), lax.axis_size("seq")
    rows = tokens.shape[0]
    count = rows // SPAN
    seq_bits = seqs.bit_length() - 1
    weights = level_weight.reshape(-1, rows).T
    square = (HEAD, HEAD)
    vmem = pl.BlockSpec(memory_space=pltpu.VMEM)
    hbm = pl.BlockSpec(memory_space=pl.ANY)
    sems = pltpu.SemaphoreType.DMA((slots_needed(seqs),))
    return pl.pallas_call(
        functools.partial(layer_kernel, groups, seqs),
        out_shape=jax.ShapeDtypeStruct((rows, w_out.shape[1]), jnp.bfloat16),
        in_specs=[hbm, hbm, hbm, vmem],
        out_specs=vmem,
        scratch_shapes=[
            pltpu.VMEM(tokens.shape, jnp.bfloat16),
            pltpu.VMEM((seqs, w_qkv.shape[0], 2 * HEADS * HEAD), jnp.bfloat16),
            pltpu.VMEM((seqs, w_qkv.shape[0], HEADS * HEAD), jnp.bfloat16),
            pltpu.VMEM((seqs, *w_out.shape), jnp.bfloat16),
            pltpu.VMEM((rows, 2 * HEADS * HEAD), jnp.float32),
            pltpu.VMEM((rows, w_qkv.shape[1]), jnp.bfloat16),
            pltpu.VMEM((count, HEADS, SPAN, SPAN), jnp.float32),
            pltpu.VMEM((rows, HEADS * HEAD), jnp.float32),
            pltpu.VMEM((rows, HEADS * HEAD), jnp.bfloat16),
            pltpu.VMEM((HEADS, *square), jnp.float32),
            pltpu.VMEM((HEADS, *square), jnp.bfloat16),
            pltpu.VMEM((HEADS, *square), jnp.bfloat16),
            pltpu.VMEM((2, *square), jnp.float32),
            pltpu.VMEM((2, *square), jnp.bfloat16),
            pltpu.VMEM((seq_bits, *square), jnp.bfloat16),
            pltpu.VMEM((seq_bits, HEADS, *square), jnp.bfloat16),
            pltpu.SemaphoreType.DMA((4,)),
            sems, sems, sems, sems, sems, sems,
            pltpu.SemaphoreType.DMA((8 * seq_bits,)),
            pltpu.SemaphoreType.DMA((8 * seq_bits,)),
        ],
        compiler_params=pltpu.CompilerParams(
            collective_id=0, has_side_effects=True, vmem_limit_bytes=63 * 1024 * 1024
        ),
    )(tokens, w_qkv, w_out, weights)


def solution(mesh):
    return jax.shard_map(
        on_device,
        mesh=mesh,
        in_specs=(
            P(("group", "seq"), None),
            P("seq", None),
            P("seq", None),
            P(None, None, ("group", "seq")),
        ),
        out_specs=P(("group", "seq"), None),
        check_vma=False,
    )
```

```python
import functools
import math

import jax
import jax.numpy as jnp
from jax import lax
from jax.experimental import pallas as pl
from jax.experimental.pallas import tpu as pltpu
from jax.sharding import PartitionSpec as P

HEADS = 4
HEAD = 256
SPAN = 256
CBITS = 8
MESH = pl.DeviceIdType.MESH


class Place:
    def __init__(self, groups, seqs):
        self.seqs = seqs
        self.chips = seqs // 2
        self.has_x = groups % 2 == 0
        self.g = lax.axis_index("group")
        self.me = lax.axis_index("seq")
        self.core = lax.rem(self.me, 2)
        self.chip = self.me // 2
        odd = lax.rem(self.chip, 2)
        half = self.chip // 2
        self.pos = half + odd * (self.chips - 1 - 2 * half)
        self.par = lax.rem(self.g, 2)
        self.mate = (self.g, self.me + 1 - 2 * self.core)
        self.cross = (self.g + 1 - 2 * self.par, self.me)

    def chip_at(self, offset):
        pos = lax.rem(self.pos + offset + self.chips, self.chips)
        late = pos // (self.chips // 2)
        return 2 * pos + late * (2 * (self.chips - 1) + 1 - 4 * pos)

    def ring(self, offset):
        return (self.g, self.chip_at(offset) * 2 + self.core)

    def flip(self, bit):
        return (self.g, self.me + (1 - 2 * self.digit(bit)) * 2**bit)

    def digit(self, bit):
        return lax.rem(self.me // 2**bit, 2)

    def greet(self, others):
        barrier = pltpu.get_barrier_semaphore()
        for other in others:
            pl.semaphore_signal(barrier, inc=1, device_id=other, device_id_type=MESH)
        pl.semaphore_wait(barrier, len(others))

    def neighbours(self):
        found = [self.ring(1), self.ring(-1), self.mate]
        return found + [self.cross] if self.has_x else found


def relay_columns(columns, has_x, share):
    return (columns * share // 8) // 128 * 128 if has_x else 0


class Gather:
    def __init__(self, place, buf, send_sem, recv_sem, share):
        self.at = place
        self.buf = buf
        self.send_sem, self.recv_sem = send_sem, recv_sem
        _, self.rows, self.columns = buf.shape
        self.sub = 2 if self.rows % 32 == 0 else 1
        self.part = self.rows // self.sub
        self.rel = relay_columns(self.columns, place.has_x, share)
        self.slots, self.sent = {}, []
        keep = self.columns - self.rel
        self.ring_cols = (place.par * self.rel, keep) if self.rel else (0, keep)
        self.give_cols = (place.par * keep, self.rel)
        self.take_cols = ((1 - place.par) * keep, self.rel)
        self.last = place.chips // 2

    def view(self, index, h, cols):
        start, width = cols
        if not isinstance(start, int):
            start = pl.multiple_of(start, 128)
        return self.buf.at[index, pl.ds(h * self.part, self.part), pl.ds(start, width)]

    def copy(self, key, index, h, cols, device):
        slot = self.slots.setdefault(key, len(self.slots))
        ref = self.view(index, h, cols)
        return pltpu.make_async_remote_copy(
            src_ref=ref,
            dst_ref=ref,
            send_sem=self.send_sem.at[slot],
            recv_sem=self.recv_sem.at[slot],
            device_id=device,
            device_id_type=MESH,
        )

    def send(self, *args):
        one = self.copy(*args)
        one.start()
        self.sent.append(one)

    def mine(self, offset):
        return self.at.chip_at(offset) * 2 + self.at.core

    def theirs(self, offset):
        return self.at.chip_at(offset) * 2 + 1 - self.at.core

    def pieces(self, step):
        every = [(h, d) for h in range(self.sub) for d in (1, -1)]
        if step < self.last:
            return every
        return [(0, 1), (1, -1)] if self.sub == 2 else [(0, 1)]

    def begin(self):
        for h, d in self.pieces(1):
            self.send(("ring", 1, h, d), self.at.me, h, self.ring_cols, self.at.ring(d))
        for h in range(self.sub):
            self.send(("own", h), self.at.me, h, (0, self.columns), self.at.mate)

    def own(self):
        for h in range(self.sub):
            self.copy(("own", h), self.theirs(0), h, (0, self.columns), self.at.mate).wait_recv()

    def arrive(self, step):
        for h, d in self.pieces(step):
            index = self.mine(-d * step)
            self.copy(("ring", step, h, d), index, h, self.ring_cols, self.at.ring(-d)).wait_recv()
            if step < self.last and (h, d) in self.pieces(step + 1):
                self.send(("ring", step + 1, h, d), index, h, self.ring_cols, self.at.ring(d))
            if step < self.last and self.rel:
                self.send(("cross", step, h, d), index, h, self.give_cols, self.at.cross)
            self.send(("mate", step, h, d), index, h, self.ring_cols, self.at.mate)

    def complete(self, step):
        if self.rel:
            for h, d in self.pieces(step):
                index = self.mine(-d * step)
                if step < self.last:
                    self.copy(("cross", step, h, d), index, h, self.take_cols, self.at.cross).wait_recv()
                    if step + 1 == self.last and (h, d) in self.pieces(step + 1):
                        self.send(("end", h, d), index, h, self.take_cols, self.at.ring(d))
                else:
                    self.copy(("end", h, d), index, h, self.take_cols, self.at.ring(-d)).wait_recv()
                self.send(("pass", step, h, d), index, h, self.take_cols, self.at.mate)
        for h, d in self.pieces(step):
            index = self.theirs(-d * step)
            self.copy(("mate", step, h, d), index, h, self.ring_cols, self.at.mate).wait_recv()
            if self.rel:
                self.copy(("pass", step, h, d), index, h, self.take_cols, self.at.mate).wait_recv()
        return (step, -step) if step < self.last else (step,)

    def steps(self, use, before_end):
        self.own()
        use(self.at.chip_at(0))
        for step in range(1, self.last):
            self.arrive(step)
            if step > 1:
                for offset in self.complete(step - 1):
                    use(self.at.chip_at(offset))
            yield
        offsets = self.complete(self.last - 1)
        before_end()
        for offset in offsets:
            use(self.at.chip_at(offset))
        self.arrive(self.last)
        yield
        for offset in self.complete(self.last):
            use(self.at.chip_at(offset))

    def drain(self):
        for one in self.sent:
            one.wait_send()


def slots_needed(seqs):
    return 4 * seqs + 8


class Exchange:
    def __init__(self, place, left, send_sem, recv_sem):
        self.at, self.left = place, left
        self.send_sem, self.recv_sem = send_sem, recv_sem
        self.slots, self.sent = {}, []
        self.c, self.y = place.core, place.digit(1)
        self.head = 2 * self.c + self.y
        self.other = 2 * self.c + 1 - self.y
        self.mate_head = 2 * (1 - self.c) + self.y
        self.mate_other = 2 * (1 - self.c) + 1 - self.y

    def copy(self, key, src, bit, head, device):
        slot = self.slots.setdefault(key, len(self.slots))
        return pltpu.make_async_remote_copy(
            src_ref=src,
            dst_ref=self.left.at[bit, head],
            send_sem=self.send_sem.at[slot],
            recv_sem=self.recv_sem.at[slot],
            device_id=device,
            device_id_type=MESH,
        )

    def send(self, *args):
        one = self.copy(*args)
        one.start()
        self.sent.append(one)

    def forward(self, key, bit, head, device):
        self.send(key, self.left.at[bit, head], bit, head, device)

    def wait(self, key, bit, head, device):
        self.copy(key, self.left.at[bit, head], bit, head, device).wait_recv()

    def spread(self, bit):
        self.forward(("quad", bit), bit, self.head, self.at.flip(1))
        self.forward(("near", bit), bit, self.head, self.at.mate)

    def collect(self, bit):
        if bit > 1:
            self.wait(("quad", bit), bit, self.other, self.at.flip(1))
        else:
            self.wait(("across", 1), bit, self.other, self.at.flip(1))
        self.forward(("far", bit), bit, self.other, self.at.mate)
        self.wait(("near", bit), bit, self.mate_head, self.at.mate)
        self.wait(("far", bit), bit, self.mate_other, self.at.mate)

    def drain(self):
        for one in self.sent:
            one.wait_send()


def product(a, b, dims):
    return lax.dot_general(a, b, (dims, ((), ())), preferred_element_type=jnp.float32)


def head_cols(h):
    return pl.ds(h * HEAD, HEAD)


def layer_kernel(
    groups, seqs, tokens_hbm, w_ref, wo_ref, weight_ref, out_ref,
    tokens_ref, kv_buf, q_buf, wo_buf, total, qkv, mix, acc, attended, local_sum, first_sum, give, pair, pair_give,
    run_give, left, load_sem, kv_send, kv_recv, q_send, q_recv, wo_send, wo_recv, ex_send, ex_recv,
):
    place = Place(groups, seqs)
    rows_w, columns = w_ref.shape
    wide = HEADS * HEAD
    here = place.me
    loads = [
        pltpu.make_async_copy(src, dst, load_sem.at[n])
        for n, (src, dst) in enumerate(
            (
                (w_ref.at[:, pl.ds(wide, columns - wide)], kv_buf.at[here]),
                (w_ref.at[:, pl.ds(0, wide)], q_buf.at[here]),
                (wo_ref, wo_buf.at[here]),
                (tokens_hbm, tokens_ref),
            )
        )
    ]
    for one in loads:
        one.start()
    seq_bits = seqs.bit_length() - 1
    place.greet(place.neighbours() + [place.flip(b) for b in range(1, seq_bits)])
    loads[0].wait()
    gather_kv = Gather(place, kv_buf, kv_send, kv_recv, 3)
    gather_kv.begin()
    for one in loads[1:]:
        one.wait()
    gather_q = Gather(place, q_buf, q_send, q_recv, 3)
    gather_o = Gather(place, wo_buf, wo_send, wo_recv, 3)

    count = tokens_ref.shape[0] // SPAN

    @pl.loop(0, count)
    def _(c):
        rows = pl.ds(pl.multiple_of(c * SPAN, SPAN), SPAN)
        i = lax.broadcasted_iota(jnp.int32, (SPAN, SPAN), 0)
        j = lax.broadcasted_iota(jnp.int32, (SPAN, SPAN), 1)
        apart = i ^ j
        for h in range(HEADS):
            value = jnp.zeros((SPAN, SPAN), jnp.float32)
            for level in range(CBITS + 1):
                gain = 1.0 / math.sqrt(HEAD * max(1, 2 ** (level - 1)))
                column = weight_ref[rows, level * HEADS + h : level * HEADS + h + 1] * gain
                column = jnp.broadcast_to(column, (SPAN, SPAN))
                value = column if level == 0 else jnp.where(apart >= 2 ** (level - 1), column, value)
            mix[c, h] = jnp.where(i >= j, value, 0.0)

    tile = 512
    aligned = (2 * rows_w) % 128 == 0

    def user(buf, base):
        started = []

        def use(chip):
            if not aligned:
                return
            started.append(1)
            step = len(started)
            x = tokens_ref[:, pl.ds(pl.multiple_of(chip * (2 * rows_w), 128), 2 * rows_w)]

            @pl.loop(0, buf.shape[2] // tile)
            def _(t):
                cols = pl.ds(pl.multiple_of(t * tile, tile), tile)
                w = buf[pl.ds(chip * 2, 2), :, cols].reshape(2 * rows_w, tile)
                y = jnp.dot(x, w, preferred_element_type=jnp.float32)
                if step == 1:
                    total[:, cols] = y
                elif step == place.chips:
                    qkv[:, pl.ds(pl.multiple_of(base + t * tile, tile), tile)] = (total[:, cols] + y).astype(qkv.dtype)
                else:
                    total[:, cols] += y

        return use

    def at_once(buf, base):
        if aligned:
            return

        @pl.loop(0, buf.shape[2] // tile)
        def _(t):
            cols = pl.ds(pl.multiple_of(t * tile, tile), tile)
            w = buf[:, :, cols].reshape(seqs * rows_w, tile)
            y = jnp.dot(tokens_ref[...], w, preferred_element_type=jnp.float32)
            qkv[:, pl.ds(pl.multiple_of(base + t * tile, tile), tile)] = y.astype(qkv.dtype)

    for _ in gather_kv.steps(user(kv_buf, wide), gather_q.begin):
        pass
    at_once(kv_buf, wide)

    for h in range(HEADS):
        for c in range(count):
            k = qkv[pl.ds(c * SPAN, SPAN), head_cols(HEADS + h)]
            v = qkv[pl.ds(c * SPAN, SPAN), head_cols(2 * HEADS + h)]
            state = product(k, v, ((0,), (0,)))
            if c == 0:
                local_sum[h] = state
                first_sum[h] = state.astype(jnp.bfloat16)
            else:
                local_sum[h] += state
        give[h] = local_sum[h].astype(jnp.bfloat16)
    exchange = Exchange(place, left, ex_send, ex_recv)
    for h in range(HEADS):
        exchange.send(("core", h), give.at[h], 0, h, place.mate)

    def exchange_steps():
        for h in range(HEADS):
            exchange.wait(("core", h), 0, h, place.mate)
        for n in range(2):
            h = 2 * place.core + n
            pair[n] = local_sum[h] + left[0, h].astype(jnp.float32)
            pair_give[n] = pair[n].astype(jnp.bfloat16)
        y = place.digit(1)
        for n, which in enumerate((1 - y, y)):
            exchange.send(("across", n), pair_give.at[which], 1, 2 * place.core + which, place.flip(1))
        yield
        exchange.wait(("across", 0), 1, exchange.head, place.flip(1))
        running = pair[y] + left[1, exchange.head].astype(jnp.float32)
        run_give[2] = running.astype(jnp.bfloat16)
        exchange.send(("hop", 2), run_give.at[2], 2, exchange.head, place.flip(2))
        exchange.forward(("near", 1), 1, exchange.head, place.mate)
        yield
        for bit in range(2, seq_bits):
            exchange.wait(("hop", bit), bit, exchange.head, place.flip(bit))
            if bit + 1 < seq_bits:
                running = running + left[bit, exchange.head].astype(jnp.float32)
                run_give[bit + 1] = running.astype(jnp.bfloat16)
                exchange.send(("hop", bit + 1), run_give.at[bit + 1], bit + 1, exchange.head, place.flip(bit + 1))
            exchange.spread(bit)
            exchange.collect(bit - 1)
            yield
        exchange.collect(seq_bits - 1)

    stages = exchange_steps()
    for _ in gather_q.steps(user(q_buf, 0), gather_o.begin):
        next(stages, None)
    at_once(q_buf, 0)

    local_bits = count.bit_length() - 1

    def gain_of(level):
        return 1.0 / math.sqrt(SPAN * 2 ** (level - 1) * HEAD)

    def weight_of(rows, level, h):
        at = (CBITS + level) * HEADS + h
        return weight_ref[rows, at : at + 1]

    def attend(c):
        rows = pl.ds(c * SPAN, SPAN)
        for h in range(HEADS):
            q = qkv[rows, head_cols(h)]
            k = qkv[rows, head_cols(HEADS + h)]
            v = qkv[rows, head_cols(2 * HEADS + h)]
            scores = product(q, k, ((1,), (1,)))
            probs = (scores * mix[c, h]).astype(jnp.bfloat16)
            got = product(probs, v, ((1,), (0,)))
            if c > 0:
                got += product(q, first_sum[h], ((1,), (0,))) * (weight_of(rows, 1, h) * gain_of(1))
            acc[rows, head_cols(h)] = got

    def read(bit):
        level = local_bits + bit + 1
        scale = place.digit(bit).astype(jnp.float32) * gain_of(level)
        every = pl.ds(0, count * SPAN)
        for h in range(HEADS):
            got = product(qkv[:, head_cols(h)], left[bit, h], ((1,), (0,)))
            acc[:, head_cols(h)] += got * (weight_of(every, level, h) * scale)

    work = [functools.partial(attend, c) for c in range(count)]
    for _ in gather_o.steps(lambda chip: None, lambda: None):
        if work:
            work.pop(0)()
        next(stages, None)
    for one in work:
        one()
    for _ in stages:
        pass
    for bit in range(seq_bits):
        read(bit)

    attended[...] = acc[...].astype(jnp.bfloat16)

    @pl.loop(0, wo_ref.shape[1] // tile)
    def _(t):
        cols = pl.ds(pl.multiple_of(t * tile, tile), tile)
        w = wo_buf[:, :, cols].reshape(wide, tile)
        out_ref[:, cols] = jnp.dot(
            attended[...], w, preferred_element_type=jnp.float32
        ).astype(out_ref.dtype)

    for one in (gather_kv, gather_q, gather_o, exchange):
        one.drain()


def on_device(tokens, w_qkv, w_out, level_weight):
    groups, seqs = lax.axis_size("group"), lax.axis_size("seq")
    rows = tokens.shape[0]
    count = rows // SPAN
    seq_bits = seqs.bit_length() - 1
    weights = level_weight.reshape(-1, rows).T
    square = (HEAD, HEAD)
    vmem = pl.BlockSpec(memory_space=pltpu.VMEM)
    hbm = pl.BlockSpec(memory_space=pl.ANY)
    sems = pltpu.SemaphoreType.DMA((slots_needed(seqs),))
    return pl.pallas_call(
        functools.partial(layer_kernel, groups, seqs),
        out_shape=jax.ShapeDtypeStruct((rows, w_out.shape[1]), jnp.bfloat16),
        in_specs=[hbm, hbm, hbm, vmem],
        out_specs=vmem,
        scratch_shapes=[
            pltpu.VMEM(tokens.shape, jnp.bfloat16),
            pltpu.VMEM((seqs, w_qkv.shape[0], 2 * HEADS * HEAD), jnp.bfloat16),
            pltpu.VMEM((seqs, w_qkv.shape[0], HEADS * HEAD), jnp.bfloat16),
            pltpu.VMEM((seqs, *w_out.shape), jnp.bfloat16),
            pltpu.VMEM((rows, 2 * HEADS * HEAD), jnp.float32),
            pltpu.VMEM((rows, w_qkv.shape[1]), jnp.bfloat16),
            pltpu.VMEM((count, HEADS, SPAN, SPAN), jnp.float32),
            pltpu.VMEM((rows, HEADS * HEAD), jnp.float32),
            pltpu.VMEM((rows, HEADS * HEAD), jnp.bfloat16),
            pltpu.VMEM((HEADS, *square), jnp.float32),
            pltpu.VMEM((HEADS, *square), jnp.bfloat16),
            pltpu.VMEM((HEADS, *square), jnp.bfloat16),
            pltpu.VMEM((2, *square), jnp.float32),
            pltpu.VMEM((2, *square), jnp.bfloat16),
            pltpu.VMEM((seq_bits, *square), jnp.bfloat16),
            pltpu.VMEM((seq_bits, HEADS, *square), jnp.bfloat16),
            pltpu.SemaphoreType.DMA((4,)),
            sems, sems, sems, sems, sems, sems,
            pltpu.SemaphoreType.DMA((8 * seq_bits,)),
            pltpu.SemaphoreType.DMA((8 * seq_bits,)),
        ],
        compiler_params=pltpu.CompilerParams(
            collective_id=0, has_side_effects=True, vmem_limit_bytes=63 * 1024 * 1024
        ),
    )(tokens, w_qkv, w_out, weights)


def solution(mesh):
    return jax.shard_map(
        on_device,
        mesh=mesh,
        in_specs=(
            P(("group", "seq"), None),
            P("seq", None),
            P("seq", None),
            P(None, None, ("group", "seq")),
        ),
        out_specs=P(("group", "seq"), None),
        check_vma=False,
    )
```
